128 devices in a mesh: sector: 4 (over z_hi, core), op: 32 (over x, y, z_lo).
Axes of the slice: x: 4, y: 4, z: 4 (z_hi: 2, z_lo: 2; z = z_hi * 2 + z_lo), core: 2. Of those that a mesh axis runs over, the one named last changes fastest.
Arguments:
- wave: float32 [8, 768, 768], P('sector', 'op'), may hold values from -6 to 6
- onsite: float32 [8, 768, 768], P('sector', 'op'), may hold values from -2 to 2
- left_ops: float32 [8, 64, 768, 768], P('sector', 'op'), may hold values from -0.21875 to 0.21875
- right_ops: float32 [8, 64, 768, 768], P('sector', 'op'), may hold values from -0.02734375 to 0.02734375
- coupling: int32 [8, 64], P('sector', 'op'), may hold values from 0 to 2
Outputs:
- sigma: float32 [8, 768, 768], P('sector', 'op')
- correction: float32 [8, 768, 768], P('sector', 'op')
The draws below stay inside these ranges and needn't reach their ends.
All inputs are finite; a program needn't handle non-finite values.
Results may differ from the reference program's by a relative error of at most 0.0001.
Values sent between devices are 32-bit elements; how exact they have to be, the bound alone decides.
A program may use at most 128 MiB of HBM per device.

```python
import jax
import jax.numpy as jnp
from jax import lax

M = 768
SECTORS = 8
PAIRS = 64


def set_ends(result, stream_key, least, top_value):
    place = [jax.random.randint(jax.random.fold_in(stream_key, axis), (), 0, length) for axis, length in enumerate(result.shape)]
    longest = result.shape.index(max(result.shape))
    next_to = place[:longest] + [(place[longest] + 1) % result.shape[longest]] + place[longest + 1:]
    return result.at[tuple(place)].set(least).at[tuple(next_to)].set(top_value)


def level_of(key, dims, cuts, low, top_value):
    loudness = 1.0
    for position, parts in cuts:
        draws = jax.random.uniform(jax.random.fold_in(jax.random.fold_in(key, 6), position), (parts,), jnp.float32, low / len(cuts), top_value / len(cuts))
        loudness = loudness * jnp.repeat(jnp.exp(draws), dims[position] // parts).reshape((-1,) + (1,) * (len(dims) - 1 - position))
    return loudness


def gaussian(own_key, shape, width, limit, shards=(), dtype=jnp.bfloat16):
    array = jax.random.normal(own_key, shape, jnp.float32) * width
    if len(shards) > 0:
        array = level_of(own_key, shape, shards, -0.22, 0.18) * array
    return jnp.clip(array, min=-limit, max=limit).astype(dtype)


def setup_inputs(seed: int = 0) -> dict:
    key_of = jax.random.split(jax.random.key(seed), 6)
    return {
        "wave": gaussian(key_of[0], (SECTORS, M, M), 1.0, 6.0, ((0, 4), (1, 32)), jnp.float32),
        "onsite": jnp.clip(jax.random.uniform(key_of[1], (SECTORS, M, M), jnp.float32, -2.0, 2.0) * level_of(key_of[1], (SECTORS, M, M), ((0, 4), (1, 32)), -0.4, 0.0), -2.0, 2.0),
        "left_ops": gaussian(key_of[2], (SECTORS, PAIRS, M, M), M ** -0.5, 0.21875, ((0, 4), (1, 32)), jnp.float32),
        "right_ops": gaussian(key_of[3], (SECTORS, PAIRS, M, M), (M * PAIRS) ** -0.5, 0.02734375, ((0, 4), (1, 32)), jnp.float32),
        "coupling": set_ends(jax.random.randint(key_of[4], (SECTORS, PAIRS), 0, 3), jax.random.fold_in(key_of[4], 1), 0, 2).astype(jnp.int32),
    }


def reference(wave, onsite, left_ops, right_ops, coupling):
    highest = lax.Precision.HIGHEST
    weights = coupling.astype(jnp.float32)
    following = jnp.roll(wave, -1, axis=0)

    def sector_terms(items):
        lefts, rights, weight, own, ahead = items

        def pair_step(acc, item):
            left, right, scale = item
            fwd = jnp.dot(jnp.dot(left, own, precision=highest), right.T, precision=highest)
            back = jnp.dot(jnp.dot(left.T, ahead, precision=highest), right, precision=highest)
            return ((acc[0] + scale * fwd, acc[1] + scale * back), None)
        zero = jnp.zeros_like(own)
        (fwd, back), _ = lax.scan(pair_step, (zero, zero), (lefts, rights, weight))
        return (fwd, back)
    forward, backward = lax.map(sector_terms, (left_ops, right_ops, weights, wave, following))
    sigma = onsite * wave + backward + jnp.roll(forward, 1, axis=0)
    total = wave.shape[0] * wave.shape[1] * wave.shape[2]
    norm_sq = jnp.sum(wave * wave)
    energy = jnp.sum(wave * sigma) / norm_sq
    gap = onsite - energy
    first = (sigma - energy * wave) * gap / jnp.maximum(gap * gap, 1.0)
    correlation = jnp.sum(wave * first)
    second = first - correlation / norm_sq * wave
    length_sq = jnp.sum(second * second)
    correction = second * lax.rsqrt(length_sq / total + 1e-06)
    return (sigma, correction)
```

```python
import functools

import jax
import jax.numpy as jnp
from jax import lax
from jax.experimental import pallas as pl
from jax.experimental.pallas import tpu as pltpu
from jax.sharding import Mesh
from jax.sharding import PartitionSpec as P

AXES = ("zh", "core", "x", "y", "zl")
SECTOR = ("zh", "core")
OP = ("x", "y", "zl")
MESH = pl.DeviceIdType.MESH
F32 = jnp.float32
BF16 = jnp.bfloat16
M = 768
RING = 4
SLAB = 48
ROWS = 24
HALF = 384
N_COPIES = 320


def split(v):
    hi = v.astype(BF16)
    return hi, (v - hi.astype(F32)).astype(BF16)


def dot3(a, b, dims):
    def one(p, q):
        return lax.dot_general(p, q, (dims, ((), ())), preferred_element_type=F32)

    return one(a[0], b[0]) + one(a[0], b[1]) + one(a[1], b[0])


NN = ((1,), (0,))
NT = ((1,), (1,))
TN = ((0,), (0,))


def fold(v):
    t = v.reshape(-1, 8, v.shape[-1]).sum(0)
    out = t[:, 0:128]
    for i in range(1, v.shape[-1] // 128):
        out = out + t[:, 128 * i : 128 * (i + 1)]
    return out


class Copies:
    def __init__(self, send, recv):
        self.send, self.recv, self.all = send, recv, []

    def new(self, src, dst, dev):
        c = Copy(self, len(self.all), src, dst, dev)
        assert c.i < N_COPIES
        self.all.append(c)
        return c


class Copy:
    def __init__(self, net, i, src, dst, dev):
        self.net, self.i, self.src, self.dst, self.dev = net, i, src, dst, dev

    def desc(self):
        return pltpu.make_async_remote_copy(
            src_ref=self.src(),
            dst_ref=self.dst(),
            send_sem=self.net.send.at[self.i],
            recv_sem=self.net.recv.at[self.i],
            device_id=self.dev,
            device_id_type=MESH,
        )

    def start(self):
        self.desc().start()

    def wait_recv(self):
        self.desc().wait_recv()

    def wait_send(self):
        self.desc().wait_send()


def kernel(
    wave, onsite, left, right, coup,
    sigma, corr,
    lh, ll, rh, rl, stage, W, uh, ul, Pb, pin, rbB, rbA, rbZ, red,
    load_sem, own_sem, send, recv,
):
    zh, core, x, y, zl = (lax.axis_index(a) for a in AXES)
    net = Copies(send, recv)
    d = 1 - 2 * core

    def at(px=None, py=None, pz=None, pc=None, ph=None):
        return (
            zh if ph is None else ph,
            core if pc is None else pc,
            x if px is None else px,
            y if py is None else py,
            zl if pz is None else pz,
        )

    def mod(v):
        return lax.rem(v + 8, RING)

    zprev = jnp.where(core == 0, 1 - zh, zh)
    zlprev = jnp.where(core == 0, 1 - zl, zl)
    prev_dev = (zprev, 1 - core, x, y, zlprev)
    znext = jnp.where(core == 1, 1 - zh, zh)
    zlnext = jnp.where(core == 1, 1 - zl, zl)
    next_dev = (znext, 1 - core, x, y, zlnext)

    barrier = pltpu.get_barrier_semaphore()
    peers = [at(px=mod(x + i)) for i in (1, 2, 3)] + [at(py=mod(y + i)) for i in (1, 2, 3)]
    cube = []
    for i in range(1, 8):
        cube.append(((zh + (i >> 2)) % 2, (core + ((i >> 1) & 1)) % 2, x, y, (zl + (i & 1)) % 2))
    peers += cube
    for p in peers:
        pl.semaphore_signal(barrier, inc=1, device_id=p, device_id_type=MESH)

    def load(i):
        src = left if i < 4 else right
        j = i % 4
        return pltpu.make_async_copy(src.at[j // 2, j % 2], stage.at[i % 3], load_sem.at[i % 3])

    order = [6, 7, 2, 3, 4, 5, 0, 1]
    loads = []
    for n, i in enumerate(order):
        src = left if i < 4 else right
        j = i % 4
        loads.append(pltpu.make_async_copy(src.at[j // 2, j % 2], stage.at[n % 3], load_sem.at[n % 3]))
    for n in range(3):
        loads[n].start()

    own = []
    for b in range(2):
        own.append(
            pltpu.make_async_copy(
                wave.at[b], W.at[b, x, y, pl.ds(pl.multiple_of(zl * ROWS, 8), ROWS), :], own_sem.at[b]
            )
        )
        own[-1].start()

    def split_op(n):
        i = order[n]
        hi_ref, lo_ref = (lh, ll) if i < 4 else (rh, rl)
        j = i % 4
        loads[n].wait()
        c = coup[j // 2, j % 2].astype(F32)

        def body(t, carry):
            rows = pl.ds(pl.multiple_of(t * 96, 16), 96)
            v = stage[n % 3, rows, :]
            if i < 4:
                v = v * c
            hi, lo = split(v)
            hi_ref[j, rows, :] = hi
            lo_ref[j, rows, :] = lo
            return carry

        lax.fori_loop(0, 8, body, 0)
        if n + 3 < 8:
            loads[n + 3].start()

    def lanes(h):
        return pl.ds(h * HALF, HALF)

    def spot(h, a, b):
        return (a, b) if h == 0 else (b, a)

    class Gather:
        def __init__(self, blk, h):
            self.blk, self.h = blk, h
            a, b = (x, y) if h == 0 else (y, x)
            self.a, self.b = a, b

            def slab(pa, pb):
                px, py = spot(h, pa, pb)
                return lambda: W.at[blk, px, py, :, lanes(h)]

            def dev(pa, pb):
                px, py = spot(h, pa, pb)
                return at(px=px, py=py)

            rows = pl.ds(pl.multiple_of(zl * ROWS, 8), ROWS)
            self.z = net.new(
                lambda: wave.at[blk, :, lanes(h)],
                lambda: W.at[blk, x, y, rows, lanes(h)],
                at(pz=1 - zl),
            )
            fa, ba = dev(mod(a + d), b), dev(mod(a - d), b)
            own_slab, from_back = slab(a, b), slab(mod(a - d), b)
            self.a1 = net.new(own_slab, own_slab, fa)
            self.a2 = net.new(own_slab, own_slab, ba)
            self.a3 = net.new(from_back, from_back, fa)
            fb, bb = dev(a, mod(b + d)), dev(a, mod(b - d))
            self.cols = []
            for o in (0, 1, 2, 3):
                pa = (a, mod(a - d), mod(a + d), mod(a + 2))[o]
                s, t = slab(pa, b), slab(pa, mod(b - d))
                self.cols.append((net.new(s, s, fb), net.new(s, s, bb), net.new(t, t, fb)))
            if blk == 0:
                def whole(pa):
                    if h == 0:
                        return (lambda: W.at[0, pa, :, :, lanes(0)]), (lambda: W.at[2, pa, :, :, lanes(0)])
                    return (lambda: W.at[0, :, pa, :, lanes(1)]), (lambda: W.at[2, :, pa, :, lanes(1)])

                self.ahead = []
                for o in range(4):
                    pa = (a, mod(a - d), mod(a + d), mod(a + 2))[o]
                    s, t = whole(pa)
                    self.ahead.append(net.new(s, t, prev_dev))

        def first(self):
            self.z.start()

        def second(self):
            self.z.wait_recv()
            self.a1.start()
            self.a2.start()
            self.spread(0)

        def spread(self, o):
            self.cols[o][0].start()
            self.cols[o][1].start()

        def third(self):
            self.a1.wait_recv()
            self.a3.start()
            self.spread(1)

        def fourth(self):
            self.a2.wait_recv()
            self.spread(2)

        def fifth(self):
            self.a3.wait_recv()
            self.spread(3)

        def relay(self, o):
            self.cols[o][0].wait_recv()
            self.cols[o][2].start()

        def finish(self, o):
            self.cols[o][1].wait_recv()
            self.cols[o][2].wait_recv()
            if self.blk == 0:
                self.ahead[o].start()

    g10, g11, g00, g01 = Gather(1, 0), Gather(1, 1), Gather(0, 0), Gather(0, 1)

    class Scatter:
        def __init__(self, blk, h):
            self.blk, self.h = blk, h
            a, b = (x, y) if h == 0 else (y, x)
            self.a, self.b = a, b
            u = blk * 2 + h

            def slab(pa, pb):
                px, py = spot(h, pa, pb)
                return lambda: Pb.at[blk, px, py, :, lanes(h)]

            def dev(pa, pb):
                px, py = spot(h, pa, pb)
                return at(px=px, py=py)

            self.slab = slab

            def buf(o, s):
                return lambda: rbB.at[u, o, s]

            def bufa(s):
                return lambda: rbA.at[u, s]

            self.rb, self.ra = (lambda o, s: rbB.at[u, o, s]), (lambda s: rbA.at[u, s])
            fb, bb = dev(a, mod(b + d)), dev(a, mod(b - d))
            self.cols = []
            for o in range(4):
                self.cols.append(
                    (
                        net.new(slab(o, mod(b + 2)), buf(o, 0), fb),
                        net.new(slab(o, mod(b - d)), buf(o, 1), bb),
                        net.new(slab(o, mod(b + d)), buf(o, 2), fb),
                    )
                )
            fa, ba = dev(mod(a + d), b), dev(mod(a - d), b)
            self.ring = (
                net.new(slab(mod(a + 2), b), bufa(0), fa),
                net.new(slab(mod(a - d), b), bufa(1), ba),
                net.new(slab(mod(a + d), b), bufa(2), fa),
            )
            other = pl.ds(pl.multiple_of((1 - zl) * ROWS, 8), ROWS)
            self.z = net.new(
                lambda: Pb.at[blk, x, y, other, lanes(h)], lambda: rbZ.at[blk, :, lanes(h)], at(pz=1 - zl)
            )

        def first(self, o):
            self.cols[o][0].start()
            self.cols[o][1].start()

        def relay(self, o):
            c = self.cols[o]
            c[0].wait_recv()
            s = self.slab(o, mod(self.b + d))()
            s[...] = s[...] + self.rb(o, 0)[...]
            c[2].start()

        def land(self, o):
            c = self.cols[o]
            c[1].wait_recv()
            c[2].wait_recv()
            s = self.slab(o, self.b)()
            s[...] = s[...] + self.rb(o, 1)[...] + self.rb(o, 2)[...]

        def ring_first(self):
            self.ring[0].start()
            self.ring[1].start()

        def ring_relay(self):
            self.ring[0].wait_recv()
            s = self.slab(mod(self.a + d), self.b)()
            s[...] = s[...] + self.ra(0)[...]
            self.ring[2].start()

        def ring_land(self):
            self.ring[1].wait_recv()
            self.ring[2].wait_recv()
            s = self.slab(self.a, self.b)()
            s[...] = s[...] + self.ra(1)[...] + self.ra(2)[...]
            self.z.start()

    s10, s11, s00, s01 = Scatter(1, 0), Scatter(1, 1), Scatter(0, 0), Scatter(0, 1)
    give = [
        net.new(
            lambda m=m: Pb.at[2, pl.ds(2 * m, 2)], lambda m=m: pin.at[pl.ds(2 * m, 2)], next_dev
        )
        for m in range(2)
    ]

    class Total:
        def __init__(self, n):
            self.n = n
            base = n * 16
            self.px, self.py, self.pz = (
                lambda i: red.at[base + i],
                lambda i: red.at[base + 4 + i],
                lambda i: red.at[base + 8 + i],
            )
            self.me = zh * 4 + core * 2 + zl
            self.cx = [net.new(lambda: self.px(x), lambda: self.px(x), at(px=mod(x + i))) for i in (1, 2, 3)]
            self.cy = [net.new(lambda: self.py(y), lambda: self.py(y), at(py=mod(y + i))) for i in (1, 2, 3)]
            self.cz = [net.new(lambda: self.pz(self.me), lambda: self.pz(self.me), p) for p in cube]

        def one(self, pair):
            r = self.px(x)
            r[...] = pair
            for c in self.cx:
                c.start()

        def two(self):
            for c in self.cx:
                c.wait_recv()
            s = self.px(0)[...]
            for i in range(1, 4):
                s = s + self.px(i)[...]
            r = self.py(y)
            r[...] = s
            for c in self.cy:
                c.start()

        def three(self):
            for c in self.cy:
                c.wait_recv()
            s = self.py(0)[...]
            for i in range(1, 4):
                s = s + self.py(i)[...]
            r = self.pz(self.me)
            r[...] = s
            for c in self.cz:
                c.start()

        def four(self):
            for c in self.cz:
                c.wait_recv()
            s = self.pz(0)[...]
            for i in range(1, 8):
                s = s + self.pz(i)[...]
            return jnp.sum(s[0], keepdims=True), jnp.sum(s[1], keepdims=True)

    def stage1(blk, j, transposed, hooks):
        def body(i, carry):
            for n, hook in enumerate(hooks):
                pl.when(i == n)(hook)
            m = lax.rem(i, 2)
            k = lax.div(i, 2)
            w = split(W[blk, pl.ds(2 * m, 2)].reshape(HALF, M))
            r = (rh[2 * j + k], rl[2 * j + k])
            u = split(dot3(w, r, NT if transposed else NN))
            rows = pl.ds(pl.multiple_of(m * HALF, HALF), HALF)
            uh[k, rows, :] = u[0]
            ul[k, rows, :] = u[1]
            return carry

        lax.fori_loop(0, 4, body, 0)

    def stage2(j, transposed, hooks, put):
        def body(m, carry):
            for n, hook in enumerate(hooks):
                pl.when(m == n)(hook)
            cut = pl.ds(pl.multiple_of(m * HALF, HALF), HALF)
            total = None
            for k in range(2):
                if transposed:
                    a = (lh[2 * j + k, :, cut], ll[2 * j + k, :, cut])
                else:
                    a = (lh[2 * j + k, cut, :], ll[2 * j + k, cut, :])
                t = dot3(a, (uh[k], ul[k]), TN if transposed else NN)
                total = t if total is None else total + t
            put(m, total.reshape(2, RING, SLAB, M))
            return carry

        lax.fori_loop(0, 2, body, 0)

    def put_to(blk):
        def put(m, v):
            Pb[blk, pl.ds(2 * m, 2)] = v

        return put

    def add_to(blk):
        def put(m, v):
            s = pl.ds(2 * m, 2)
            Pb[blk, s] = Pb[blk, s] + v

        return put

    def put_with_pin(m, v):
        s = pl.ds(2 * m, 2)
        Pb[0, s] = pin[s] + v

    def inner(wblk, pblk):
        def body(i, acc):
            return acc + fold((W[wblk, i] * Pb[pblk, i]).reshape(RING * SLAB, M))

        return lax.fori_loop(0, 4, body, jnp.zeros((8, 128), F32))

    pl.semaphore_wait(barrier, len(peers))
    for g in (g10, g11, g00, g01):
        g.first()
    split_op(0)
    own[0].wait()
    own[1].wait()
    g10.second()
    g11.second()
    split_op(1)
    for s in ("third", "fourth"):
        getattr(g10, s)()
        getattr(g11, s)()
    split_op(2)
    g10.relay(0)
    g11.relay(0)
    g10.fifth()
    g11.fifth()
    g00.second()
    g01.second()
    split_op(3)
    for o in (1, 2, 3):
        g10.relay(o)
        g11.relay(o)
    split_op(4)
    for s in ("third", "fourth"):
        getattr(g00, s)()
        getattr(g01, s)()
    split_op(5)
    g00.relay(0)
    g01.relay(0)
    g00.fifth()
    g01.fifth()
    for o in (0, 1, 2, 3):
        g10.finish(o)
        g11.finish(o)

    def both(fn):
        return lambda: (fn(g00), fn(g01), None)[2]

    stage1(
        1, 1, True,
        [both(lambda g: g.relay(1)), both(lambda g: g.relay(2)), both(lambda g: g.relay(3)), both(lambda g: g.finish(0))],
    )
    stage2(1, False, [both(lambda g: g.finish(1)), both(lambda g: g.finish(2))], put_to(2))
    give[0].start()
    give[1].start()
    g00.finish(3)
    g01.finish(3)
    split_op(6)
    split_op(7)
    stage1(0, 0, True, [])
    stage2(0, False, [], put_to(1))
    for g in (g00, g01):
        for o in range(4):
            g.ahead[o].wait_recv()
    w01 = [wave[b] for b in range(2)]
    pp = fold(w01[0] * w01[0]) + fold(w01[1] * w01[1])
    ps = fold(onsite[0] * w01[0] * w01[0]) + fold(onsite[1] * w01[1] * w01[1])
    ps = ps + 2.0 * (inner(1, 1) + inner(2, 2))
    t0, t1 = Total(0), Total(1)
    t0.one(jnp.stack([pp, ps]))
    stage1(2, 1, False, [lambda: None, t0.two])
    stage2(1, True, [t0.three], add_to(1))

    pair1 = (s10, s11)
    for s in pair1:
        for o in range(4):
            s.first(o)

    def on(pair, fn):
        return lambda: (fn(pair[0]), fn(pair[1]), None)[2]

    stage1(
        1, 0, False,
        [
            lambda: None,
            on(pair1, lambda s: (s.relay(0), s.relay(1))),
            on(pair1, lambda s: (s.relay(2), s.relay(3))),
            lambda: None,
        ],
    )
    for g in give:
        g.wait_recv()
    for s in pair1:
        for o in range(4):
            s.land(o)
        s.ring_first()
    stage2(0, True, [lambda: None, on(pair1, lambda s: s.ring_relay())], put_with_pin)
    pair0 = (s00, s01)
    for s in pair0:
        for o in range(4):
            s.first(o)
    for s in pair1:
        s.ring_land()
    for o in range(4):
        for s in pair0:
            s.relay(o)
    norm_sq, energy_sum = t0.four()
    energy = energy_sum / norm_sq
    for o in range(4):
        for s in pair0:
            s.land(o)
    for s in pair0:
        s.ring_first()
    for s in pair0:
        s.ring_relay()
    for s in pair0:
        s.ring_land()
    mine = pl.ds(pl.multiple_of(zl * ROWS, 8), ROWS)
    pt = jnp.zeros((8, 128), F32)
    tt = jnp.zeros((8, 128), F32)
    for b in (1, 0):
        for s in (s10, s11) if b == 1 else pair0:
            s.z.wait_recv()
        w = wave[b]
        sig = onsite[b] * w + Pb[b, x, y, mine, :] + rbZ[b]
        sigma[b] = sig
        gap = onsite[b] - energy
        first = (sig - energy * w) * gap / jnp.maximum(gap * gap, 1.0)
        corr[b] = first
        pt = pt + fold(w * first)
        tt = tt + fold(first * first)
    t1.one(jnp.stack([pt, tt]))
    t1.two()
    t1.three()
    correlation, first_sq = t1.four()
    ratio = correlation / norm_sq
    length_sq = first_sq - correlation * ratio
    scale = lax.rsqrt(length_sq / float(8 * M * M) + 1e-06)
    for b in range(2):
        corr[b] = (corr[b] - ratio * wave[b]) * scale
    for c in net.all:
        c.wait_send()


def solution(mesh):
    finer = Mesh(mesh.devices.reshape(2, 2, 4, 4, 2), AXES)
    block = P(SECTOR, OP, None)
    ops = P(SECTOR, OP, None, None)

    def step(wave, onsite, left, right, coupling):
        vm = pl.BlockSpec(memory_space=pltpu.VMEM)
        anyw = pl.BlockSpec(memory_space=pl.ANY)
        shape = jax.ShapeDtypeStruct((2, ROWS, M), F32)
        return pl.pallas_call(
            kernel,
            out_shape=(shape, shape),
            in_specs=[vm, vm, anyw, anyw, pl.BlockSpec(memory_space=pltpu.SMEM)],
            out_specs=(vm, vm),
            scratch_shapes=[
                pltpu.VMEM((4, M, M), BF16),
                pltpu.VMEM((4, M, M), BF16),
                pltpu.VMEM((4, M, M), BF16),
                pltpu.VMEM((4, M, M), BF16),
                pltpu.VMEM((3, M, M), F32),
                pltpu.VMEM((3, RING, RING, SLAB, M), F32),
                pltpu.VMEM((2, M, M), BF16),
                pltpu.VMEM((2, M, M), BF16),
                pltpu.VMEM((3, RING, RING, SLAB, M), F32),
                pltpu.VMEM((RING, RING, SLAB, M), F32),
                pltpu.VMEM((4, 4, 3, SLAB, HALF), F32),
                pltpu.VMEM((4, 3, SLAB, HALF), F32),
                pltpu.VMEM((2, ROWS, M), F32),
                pltpu.VMEM((32, 2, 8, 128), F32),
                pltpu.SemaphoreType.DMA((3,)),
                pltpu.SemaphoreType.DMA((2,)),
                pltpu.SemaphoreType.DMA((N_COPIES,)),
                pltpu.SemaphoreType.DMA((N_COPIES,)),
            ],
            compiler_params=pltpu.CompilerParams(
                collective_id=0, has_side_effects=True, vmem_limit_bytes=67043328
            ),
        )(wave, onsite, left, right, coupling)

    return jax.shard_map(
        step,
        mesh=finer,
        in_specs=(block, block, ops, ops, P(SECTOR, OP)),
        out_specs=(block, block),
        check_vma=False,
    )
```

```python
import functools

import jax
import jax.numpy as jnp
from jax import lax
from jax.experimental import pallas as pl
from jax.experimental.pallas import tpu as pltpu
from jax.sharding import Mesh
from jax.sharding import PartitionSpec as P

AXES = ("zh", "core", "x", "y", "zl")
SECTOR = ("zh", "core")
OP = ("x", "y", "zl")
MESH = pl.DeviceIdType.MESH
F32 = jnp.float32
BF16 = jnp.bfloat16
M = 768
RING = 4
SLAB = 48
ROWS = 24
HALF = 384
N_SEND = 7
N_RECV = 112


def split(v):
    hi = v.astype(BF16)
    return hi, (v - hi.astype(F32)).astype(BF16)


def dot3(a, b, dims):
    def one(p, q):
        return lax.dot_general(p, q, (dims, ((), ())), preferred_element_type=F32)

    return one(a[0], b[0]) + one(a[0], b[1]) + one(a[1], b[0])


NN = ((1,), (0,))
NT = ((1,), (1,))
TN = ((0,), (0,))


def fold(v):
    t = v.reshape(-1, 8, v.shape[-1]).sum(0)
    out = t[:, 0:128]
    for i in range(1, v.shape[-1] // 128):
        out = out + t[:, 128 * i : 128 * (i + 1)]
    return out


class Copies:
    def __init__(self, send, recv):
        self.send, self.recv, self.got = send, recv, 0

    def new_recv(self):
        assert self.got < N_RECV
        self.got += 1
        return self.got - 1

    def new(self, src, dst, dev, group, got=None, sends=None, gets=None):
        return Copy(self, src, dst, dev, group, self.new_recv() if got is None else got, sends, gets)


class Copy:
    def __init__(self, net, src, dst, dev, group, got, sends, gets):
        self.net, self.src, self.dst, self.dev = net, src, dst, dev
        self.group, self.got, self.sends, self.gets = group, got, sends, gets

    def desc(self):
        return pltpu.make_async_remote_copy(
            src_ref=self.src(),
            dst_ref=self.dst(),
            send_sem=self.net.send.at[self.group],
            recv_sem=self.net.recv.at[self.got],
            device_id=self.dev,
            device_id_type=MESH,
        )

    def under(self, cond, act):
        if cond is None:
            act(self.desc())
        else:
            pl.when(cond)(lambda: act(self.desc()))

    def start(self):
        self.under(self.sends, lambda c: c.start())

    def wait_recv(self):
        self.under(self.gets, lambda c: c.wait_recv())


def wait_bytes(sem, like):
    pltpu.make_async_copy(like, like, sem).wait()


def kernel(
    wave, onsite, left, right, coup,
    psum_out, first_out, ratio_out, scale_out,
    lh, ll, rh, rl, stage, W, uh, ul, Pb, pin, zin, rbB, rbZ, red, wv, on_, ob,
    load_sem, own_sem, in_sem, out_sem, send, recv,
):
    zh, core, x, y, zl = (lax.axis_index(a) for a in AXES)
    net = Copies(send, recv)
    d = 1 - 2 * core

    def at(px=None, py=None, pz=None):
        return (zh, core, x if px is None else px, y if py is None else py, zl if pz is None else pz)

    def mod(v):
        return lax.rem(v + 8, RING)

    zprev = jnp.where(core == 0, 1 - zh, zh)
    zlprev = jnp.where(core == 0, 1 - zl, zl)
    prev_dev = (zprev, 1 - core, x, y, zlprev)
    znext = jnp.where(core == 1, 1 - zh, zh)
    zlnext = jnp.where(core == 1, 1 - zl, zl)
    next_dev = (znext, 1 - core, x, y, zlnext)

    barrier = pltpu.get_barrier_semaphore()
    peers = []
    for i in (1, 2, 3):
        for o in (0, 1):
            peers.append(at(px=mod(x + i), pz=(zl + o) % 2))
            peers.append(at(py=mod(y + i), pz=(zl + o) % 2))
    cube = []
    for i in range(1, 8):
        cube.append(((zh + (i >> 2)) % 2, (core + ((i >> 1) & 1)) % 2, x, y, (zl + (i & 1)) % 2))
    for i in (1, 2, 3):
        for k in (1, 2, 3):
            peers.append(at(px=mod(x + i), py=mod(y + k)))
    peers += cube
    for p in peers:
        pl.semaphore_signal(barrier, inc=1, device_id=p, device_id_type=MESH)

    own = []
    for b in range(2):
        own.append(
            pltpu.make_async_copy(
                wave.at[b], W.at[b, x, y, pl.ds(pl.multiple_of(zl * ROWS, 8), ROWS), :], own_sem.at[b]
            )
        )
        own[-1].start()

    order = [4, 5, 0, 1, 6, 7, 2, 3]
    loads = []
    for n, i in enumerate(order):
        src = left if i < 4 else right
        j = i % 4
        loads.append(pltpu.make_async_copy(src.at[j // 2, j % 2], stage.at[n % 3], load_sem.at[n % 3]))
    for n in range(3):
        loads[n].start()
    fetch = [
        pltpu.make_async_copy(wave, wv, in_sem.at[0]),
        pltpu.make_async_copy(onsite, on_, in_sem.at[1]),
    ]
    for c in fetch:
        c.start()

    def split_op(n):
        i = order[n]
        hi_ref, lo_ref = (lh, ll) if i < 4 else (rh, rl)
        j = i % 4
        loads[n].wait()
        c = coup[j // 2, j % 2].astype(F32)

        def body(t, carry):
            rows = pl.ds(pl.multiple_of(t * 96, 16), 96)
            v = stage[n % 3, rows, :]
            if i < 4:
                v = v * c
            hi, lo = split(v)
            hi_ref[j, rows, :] = hi
            lo_ref[j, rows, :] = lo
            return carry

        lax.fori_loop(0, 8, body, 0)
        if n + 3 < 8:
            loads[n + 3].start()

    def lanes(h):
        return pl.ds(h * HALF, HALF)

    def spot(h, a, b):
        return (a, b) if h == 0 else (b, a)

    def rows_of(z):
        return pl.ds(pl.multiple_of(z * ROWS, 8), ROWS)

    ahead_got = net.new_recv()

    class Gather:
        def __init__(self, blk, h):
            self.blk, self.h = blk, h
            a, b = (x, y) if h == 0 else (y, x)

            def slab(pa, pb):
                px, py = spot(h, pa, pb)
                return lambda: W.at[blk, px, py, :, lanes(h)]

            def dev(pa, pb, z=None):
                px, py = spot(h, pa, pb)
                return at(px=px, py=py, pz=z)

            self.near, self.got = {}, []
            for i in range(4):
                self.got.append(net.new_recv())
                for o in (1, 0):
                    if (i, o) != (0, 0):
                        self.near[i, o] = net.new(
                            lambda: wave.at[blk, :, lanes(h)],
                            lambda: W.at[blk, x, y, rows_of(zl), lanes(h)],
                            dev(mod(a + i), b, (zl + o) % 2),
                            0,
                            self.got[i],
                        )
            fb, bb = dev(a, mod(b + d)), dev(a, mod(b - d))
            self.cols, self.ahead = [], []
            for o in range(4):
                pa = mod(a - o)
                s, t = slab(pa, b), slab(pa, mod(b - d))
                self.cols.append((net.new(s, s, fb, 1), net.new(s, s, bb, 1), net.new(t, t, fb, 1)))
                if blk == 0:
                    on = []
                    for pb in (b, mod(b - d), mod(b + d), mod(b + 2)):
                        px, py = spot(h, pa, pb)

                        def src(px=px, py=py):
                            return W.at[0, px, py, :, lanes(h)]

                        def dst(px=px, py=py):
                            return W.at[2, px, py, :, lanes(h)]

                        on.append(net.new(src, dst, prev_dev, 2, ahead_got))
                    self.ahead.append(on)

        def pass_on(self, o, s):
            if self.blk == 0:
                self.ahead[o][s].start()

        def spread(self, o):
            if o == 0:
                self.near[0, 1].wait_recv()
            else:
                wait_bytes(recv.at[self.got[o]], rbB.at[0, 0, 0])
            self.cols[o][0].start()
            self.cols[o][1].start()
            self.pass_on(o, 0)

        def relay(self, o):
            self.cols[o][0].wait_recv()
            self.cols[o][2].start()
            self.pass_on(o, 1)

        def finish(self, o):
            self.cols[o][1].wait_recv()
            self.pass_on(o, 2)
            self.cols[o][2].wait_recv()
            self.pass_on(o, 3)

    g10, g11, g00, g01 = Gather(1, 0), Gather(1, 1), Gather(0, 0), Gather(0, 1)

    def step1(pair):
        for i in (0, 1, 3, 2):
            for o in (1, 0):
                if (i, o) != (0, 0):
                    for g in pair:
                        g.near[i, o].start()

    class Scatter:
        def __init__(self, blk, h):
            self.blk, self.h = blk, h
            a, b = (x, y) if h == 0 else (y, x)
            self.a, self.b = a, b
            u = blk * 2 + h
            self.u = u

            def slab(pa, pb):
                px, py = spot(h, pa, pb)
                return lambda: Pb.at[blk, px, py, :, lanes(h)]

            def dev(pa, pb, z=None):
                px, py = spot(h, pa, pb)
                return at(px=px, py=py, pz=z)

            self.slab = slab

            def buf(o, s):
                return lambda: rbB.at[u, o, s]

            self.rb = lambda o, s: rbB.at[u, o, s]
            fb, bb = dev(a, mod(b + d)), dev(a, mod(b - d))
            self.cols = []
            for o in range(4):
                both = net.new_recv()
                self.cols.append(
                    (
                        net.new(slab(o, mod(b + 2)), buf(o, 0), fb, 3),
                        net.new(slab(o, mod(b - d)), buf(o, 1), bb, 3, both),
                        net.new(slab(o, mod(b + d)), buf(o, 2), fb, 3, both),
                        both,
                    )
                )
            self.near, self.got = [], net.new_recv()
            for i in (2, 1, 3, 0):
                for o in (1, 0):
                    if (i, o) != (0, 0):
                        px, py = spot(h, mod(a + i), b)
                        z = (zl + o) % 2

                        def src(px=px, py=py, z=z):
                            return Pb.at[blk, px, py, rows_of(z), lanes(h)]

                        def dst(k=i * 2 + o):
                            return rbZ.at[u, k]

                        self.near.append(net.new(src, dst, dev(mod(a + i), b, z), 4, self.got))

        def first(self, o, half=None):
            c = self.cols[o]
            if half is None or self.h == 0:
                if half is None or o // 2 == half:
                    c[0].start()
                    c[1].start()
            else:
                pl.when(lax.div(mod(self.b + 2), 2) == half)(c[0].start)
                pl.when(lax.div(mod(self.b - d), 2) == half)(c[1].start)

        def relay(self, o):
            c = self.cols[o]
            c[0].wait_recv()
            s = self.slab(o, mod(self.b + d))()
            s[...] = s[...] + self.rb(o, 0)[...]
            c[2].start()

        def land(self, o):
            c = self.cols[o]
            wait_bytes(recv.at[c[3]], rbB.at[self.u, o, pl.ds(1, 2)])
            s = self.slab(o, self.b)()
            s[...] = s[...] + self.rb(o, 1)[...] + self.rb(o, 2)[...]

        def last(self):
            for c in self.near:
                c.start()

        def result(self):
            wait_bytes(recv.at[self.got], rbZ.at[self.u, pl.ds(1, 7)])
            t = Pb[self.blk, x, y, rows_of(zl), lanes(self.h)]
            for k in range(1, 8):
                t = t + rbZ[self.u, k]
            return t

    s10, s11, s00, s01 = Scatter(1, 0), Scatter(1, 1), Scatter(0, 0), Scatter(0, 1)

    ex = [
        net.new((lambda q=q: Pb.at[2, (1 - zl) * 2 + q]), (lambda q=q: zin.at[q]), at(pz=1 - zl), 5, sends=core == 1)
        for q in range(2)
    ]
    pin_got = net.new_recv()
    far = [
        net.new((lambda q=q: Pb.at[2, zl * 2 + q]), (lambda q=q: pin.at[zl * 2 + q]), next_dev, 5, pin_got)
        for q in range(2)
    ]
    chip = [
        net.new((lambda q=q: Pb.at[2, q]), (lambda q=q: pin.at[q]), next_dev, 5, pin_got, sends=core == 0)
        for q in range(4)
    ]

    def take_pin():
        pl.when(core == 1)(lambda: wait_bytes(recv.at[pin_got], pin))
        pl.when(core == 0)(lambda: wait_bytes(recv.at[pin_got], pin.at[pl.ds(0, 2)]))

    def give():
        for c in ex + chip:
            c.start()

    def fold_pair(q):
        @pl.when(core == 1)
        def _():
            ex[q].desc().wait_recv()
            i = zl * 2 + q
            Pb[2, i] = Pb[2, i] + zin[q]
            far[q].desc().start()

    plane = []
    for i in range(RING):
        for k in range(RING):
            if (i, k) != (0, 0):
                plane.append(at(px=mod(x + i), py=mod(y + k)))
    GX = ([at(px=mod(x + i)) for i in (1, 2, 3)], x)
    GY = ([at(py=mod(y + i)) for i in (1, 2, 3)], y)
    GC = (cube, zh * 4 + core * 2 + zl)
    GP = (plane, x * RING + y)

    class Total:
        def __init__(self, base, groups):
            self.stages = []
            for devs, me in groups:
                n = len(devs) + 1
                got = net.new_recv()

                def spot_of(base=base, me=me):
                    return red.at[base + me]

                copies = [net.new(spot_of, spot_of, p, 6, got) for p in devs]
                self.stages.append((base, n, spot_of, copies, got))
                base += n
            self.end = base

        def put(self, k, pair):
            _, _, spot_of, copies, _ = self.stages[k]
            r = spot_of()
            r[...] = pair
            for c in copies:
                c.start()

        def get(self, k):
            base, n, _, copies, got = self.stages[k]
            wait_bytes(recv.at[got], red.at[pl.ds(0, n - 1)])
            s = red[base]
            for i in range(1, n):
                s = s + red[base + i]
            return s

        def step(self, k):
            self.put(k + 1, self.get(k))

        def done(self):
            s = self.get(len(self.stages) - 1)
            return jnp.sum(s[0], keepdims=True), jnp.sum(s[1], keepdims=True)

    def stage1(blk, j, transposed, hooks):
        def body(i, carry):
            for n, hook in enumerate(hooks):
                pl.when(i == n)(hook)
            m = lax.rem(i, 2)
            k = lax.div(i, 2)
            w = split(W[blk, pl.ds(2 * m, 2)].reshape(HALF, M))
            r = (rh[2 * j + k], rl[2 * j + k])
            u = split(dot3(w, r, NT if transposed else NN))
            rows = pl.ds(pl.multiple_of(m * HALF, HALF), HALF)
            uh[k, rows, :] = u[0]
            ul[k, rows, :] = u[1]
            return carry

        lax.fori_loop(0, 4, body, 0)

    def stage2(j, transposed, hooks, put):
        def body(m, carry):
            for n, hook in enumerate(hooks):
                pl.when(m == n)(hook)
            cut = pl.ds(pl.multiple_of(m * HALF, HALF), HALF)
            total = None
            for k in range(2):
                if transposed:
                    a = (lh[2 * j + k, :, cut], ll[2 * j + k, :, cut])
                else:
                    a = (lh[2 * j + k, cut, :], ll[2 * j + k, cut, :])
                t = dot3(a, (uh[k], ul[k]), TN if transposed else NN)
                total = t if total is None else total + t
            put(m, total.reshape(2, RING, SLAB, M))
            return carry

        lax.fori_loop(0, 2, body, 0)

    def put_to(blk):
        def put(m, v):
            Pb[blk, pl.ds(2 * m, 2)] = v

        return put

    def add_to(blk):
        def put(m, v):
            s = pl.ds(2 * m, 2)
            Pb[blk, s] = Pb[blk, s] + v

        return put

    def put_with_pin(m, v):
        s = pl.ds(2 * m, 2)
        Pb[0, s] = v

        @pl.when((core == 1) | (m == 1 - zl))
        def _():
            Pb[0, s] = Pb[0, s] + pin[s]

    def inner(wblk, pblk):
        def body(i, acc):
            return acc + fold((W[wblk, i] * Pb[pblk, i]).reshape(RING * SLAB, M))

        return lax.fori_loop(0, 4, body, jnp.zeros((8, 128), F32))

    def on(pair, fn):
        def run():
            for g in pair:
                fn(g)

        return run

    def chain(*fns):
        def run():
            for f in fns:
                f()

        return run

    G0, G1, S1, S0 = (g00, g01), (g10, g11), (s10, s11), (s00, s01)
    pl.semaphore_wait(barrier, len(peers))
    step1(G0)
    own[0].wait()
    own[1].wait()
    split_op(0)
    on(G0, lambda g: g.spread(0))()
    split_op(1)
    for o in (1, 3, 2):
        on(G0, lambda g: g.spread(o))()
    split_op(2)
    on(G0, lambda g: g.relay(0))()
    split_op(3)
    on(G0, lambda g: g.relay(1))()
    split_op(4)
    on(G0, lambda g: g.relay(3))()
    split_op(5)
    on(G0, lambda g: g.relay(2))()
    step1(G1)
    split_op(6)
    split_op(7)
    for o in (0, 1, 3, 2):
        on(G0, lambda g: g.finish(o))()

    def none():
        pass

    stage1(
        0, 0, True,
        [
            lambda: on(G1, lambda g: g.spread(0))(),
            lambda: on(G1, lambda g: (g.spread(1), g.spread(3)))(),
            lambda: on(G1, lambda g: g.spread(2))(),
            on(G1, lambda g: (g.relay(0), g.relay(1))),
        ],
    )
    stage2(0, False, [on(G1, lambda g: g.relay(3)), on(G1, lambda g: g.relay(2))], put_to(1))
    for o in range(4):
        on(G1, lambda g: g.finish(o))()
    stage1(1, 1, True, [])
    stage2(1, False, [], put_to(2))
    give()
    wait_bytes(recv.at[ahead_got], W.at[2])
    for c in fetch:
        c.wait()
    pp = fold(wv[0] * wv[0]) + fold(wv[1] * wv[1])
    ps = fold(on_[0] * wv[0] * wv[0]) + fold(on_[1] * wv[1] * wv[1])
    ps = ps + 2.0 * (inner(1, 1) + inner(2, 2))
    t0 = Total(0, (GX, GY, GC))
    t1 = Total(16, (GP, GC))
    t0.put(0, jnp.stack([pp, ps]))
    stage1(2, 1, False, [])

    def send_half(pair, half):
        for s in pair:
            for o in range(4):
                s.first(o, half)

    stage2(
        1, True,
        [lambda: (fold_pair(0), t0.step(0), None)[2], lambda: send_half(S1, 0)],
        add_to(1),
    )
    send_half(S1, 1)
    stage1(
        1, 0, False,
        [
            lambda: fold_pair(1),
            lambda: t0.step(1),
            on(S1, lambda s: (s.relay(0), s.relay(1))),
            on(S1, lambda s: s.relay(2)),
        ],
    )
    take_pin()

    def land(pair, cols):
        for o in cols:
            for s in pair:
                s.land(o)

    stage2(
        0, True,
        [
            on(S1, lambda s: s.relay(3)),
            chain(lambda: send_half(S0, 0), lambda: land(S1, (0, 1))),
        ],
        put_with_pin,
    )
    send_half(S0, 1)
    land(S1, (2, 3))
    on(S1, lambda s: s.last())()
    norm_sq, energy_sum = t0.done()
    energy = energy_sum / norm_sq
    for o in range(4):
        on(S0, lambda s: s.relay(o))()
    land(S0, range(4))
    on(S0, lambda s: s.last())()
    pt = jnp.zeros((8, 128), F32)
    tt = jnp.zeros((8, 128), F32)
    out = []
    for b, pair in ((1, S1), (0, S0)):
        for s in pair:
            h = slice(s.h * HALF, s.h * HALF + HALF)
            w, o_ = wv[b, :, h], on_[b, :, h]
            total = s.result()
            ob[0, b, :, h] = total
            sig = o_ * w + total
            gap = o_ - energy
            first = (sig - energy * w) * gap / jnp.maximum(gap * gap, 1.0)
            ob[1, b, :, h] = first
            pt = pt + fold(w * first)
            tt = tt + fold(first * first)
        out.append(pltpu.make_async_copy(ob.at[0, b], psum_out.at[b], out_sem.at[b]))
        out.append(pltpu.make_async_copy(ob.at[1, b], first_out.at[b], out_sem.at[2 + b]))
    t1.put(0, jnp.stack([pt, tt]))
    for c in out:
        c.start()
    t1.step(0)
    correlation, first_sq = t1.done()
    ratio = correlation / norm_sq
    length_sq = first_sq - correlation * ratio
    ratio_out[...] = jnp.broadcast_to(ratio, (8, M))
    scale_out[...] = jnp.broadcast_to(lax.rsqrt(length_sq / float(8 * M * M) + 1e-06), (8, M))
    for c in out:
        c.wait()
    near28 = rbZ.at[:, pl.ds(1, 7)]
    slabs48 = Pb.at[:, :, :, :, lanes(0)]
    for group, like in enumerate((near28, slabs48, W.at[2], slabs48, near28, pin, red.at[pl.ds(0, 35)])):
        wait_bytes(send.at[group], like)


def solution(mesh):
    finer = Mesh(mesh.devices.reshape(2, 2, 4, 4, 2), AXES)
    block = P(SECTOR, OP, None)
    ops = P(SECTOR, OP, None, None)

    def step(wave, onsite, left, right, coupling):
        vm = pl.BlockSpec(memory_space=pltpu.VMEM)
        anyw = pl.BlockSpec(memory_space=pl.ANY)
        shape = jax.ShapeDtypeStruct((2, ROWS, M), F32)
        psum, first, ratio, scale = pl.pallas_call(
            kernel,
            out_shape=(shape, shape) + (jax.ShapeDtypeStruct((8, M), F32),) * 2,
            in_specs=[anyw, anyw, anyw, anyw, pl.BlockSpec(memory_space=pltpu.SMEM)],
            out_specs=(anyw, anyw, vm, vm),
            scratch_shapes=[
                pltpu.VMEM((4, M, M), BF16),
                pltpu.VMEM((4, M, M), BF16),
                pltpu.VMEM((4, M, M), BF16),
                pltpu.VMEM((4, M, M), BF16),
                pltpu.VMEM((3, M, M), F32),
                pltpu.VMEM((3, RING, RING, SLAB, M), F32),
                pltpu.VMEM((2, M, M), BF16),
                pltpu.VMEM((2, M, M), BF16),
                pltpu.VMEM((3, RING, RING, SLAB, M), F32),
                pltpu.VMEM((RING, RING, SLAB, M), F32),
                pltpu.VMEM((2, RING, SLAB, M), F32),
                pltpu.VMEM((4, 4, 3, SLAB, HALF), F32),
                pltpu.VMEM((4, 8, ROWS, HALF), F32),
                pltpu.VMEM((40, 2, 8, 128), F32),
                pltpu.VMEM((2, ROWS, M), F32),
                pltpu.VMEM((2, ROWS, M), F32),
                pltpu.VMEM((2, 2, ROWS, M), F32),
                pltpu.SemaphoreType.DMA((3,)),
                pltpu.SemaphoreType.DMA((2,)),
                pltpu.SemaphoreType.DMA((2,)),
                pltpu.SemaphoreType.DMA((4,)),
                pltpu.SemaphoreType.DMA((N_SEND,)),
                pltpu.SemaphoreType.DMA((N_RECV,)),
            ],
            compiler_params=pltpu.CompilerParams(
                collective_id=0, has_side_effects=True, vmem_limit_bytes=67043328
            ),
        )(wave, onsite, left, right, coupling)
        sigma = onsite * wave + psum
        tiles = (2, ROWS // 8, 8, M)
        second = (first.reshape(tiles) - ratio * wave.reshape(tiles)) * scale
        return sigma, second.reshape(wave.shape)

    return jax.shard_map(
        step,
        mesh=finer,
        in_specs=(block, block, ops, ops, P(SECTOR, OP)),
        out_specs=(block, block),
        check_vma=False,
    )
```

```python
import functools

import jax
import jax.numpy as jnp
from jax import lax
from jax.experimental import pallas as pl
from jax.experimental.pallas import tpu as pltpu
from jax.sharding import Mesh
from jax.sharding import PartitionSpec as P

AXES = ("zh", "core", "x", "y", "zl")
SECTOR = ("zh", "core")
OP = ("x", "y", "zl")
MESH = pl.DeviceIdType.MESH
F32 = jnp.float32
BF16 = jnp.bfloat16
M = 768
RING = 4
SLAB = 48
ROWS = 24
HALF = 384
N_SEND = 7
N_RECV = 120


def split(v):
    hi = v.astype(BF16)
    return hi, (v - hi.astype(F32)).astype(BF16)


def dot3(a, b, dims):
    def one(p, q):
        return lax.dot_general(p, q, (dims, ((), ())), preferred_element_type=F32)

    return one(a[0], b[0]) + one(a[0], b[1]) + one(a[1], b[0])


NN = ((1,), (0,))
NT = ((1,), (1,))
TN = ((0,), (0,))


def fold(v):
    t = v.reshape(-1, 8, v.shape[-1]).sum(0)
    out = t[:, 0:128]
    for i in range(1, v.shape[-1] // 128):
        out = out + t[:, 128 * i : 128 * (i + 1)]
    return out


class Copies:
    def __init__(self, send, recv):
        self.send, self.recv, self.got = send, recv, 0

    def new_recv(self):
        assert self.got < N_RECV
        self.got += 1
        return self.got - 1

    def new(self, src, dst, dev, group, got=None, sends=None, gets=None):
        return Copy(self, src, dst, dev, group, self.new_recv() if got is None else got, sends, gets)


class Copy:
    def __init__(self, net, src, dst, dev, group, got, sends, gets):
        self.net, self.src, self.dst, self.dev = net, src, dst, dev
        self.group, self.got, self.sends, self.gets = group, got, sends, gets

    def desc(self):
        return pltpu.make_async_remote_copy(
            src_ref=self.src(),
            dst_ref=self.dst(),
            send_sem=self.net.send.at[self.group],
            recv_sem=self.net.recv.at[self.got],
            device_id=self.dev,
            device_id_type=MESH,
        )

    def under(self, cond, act):
        if cond is None:
            act(self.desc())
        else:
            pl.when(cond)(lambda: act(self.desc()))

    def start(self):
        self.under(self.sends, lambda c: c.start())

    def wait_recv(self):
        self.under(self.gets, lambda c: c.wait_recv())


def wait_bytes(sem, like):
    pltpu.make_async_copy(like, like, sem).wait()


def kernel(
    wave, onsite, left, right, coup,
    psum_out, first_out, ratio_out, scale_out,
    lh, ll, rh, rl, stage, W, uh, ul, Pb, pin, zin, rbB, rbZ, red, wv, on_, ob,
    load_sem, own_sem, in_sem, out_sem, send, recv,
):
    zh, core, x, y, zl = (lax.axis_index(a) for a in AXES)
    net = Copies(send, recv)
    d = 1 - 2 * core

    def at(px=None, py=None, pz=None):
        return (zh, core, x if px is None else px, y if py is None else py, zl if pz is None else pz)

    def mod(v):
        return lax.rem(v + 8, RING)

    zprev = jnp.where(core == 0, 1 - zh, zh)
    zlprev = jnp.where(core == 0, 1 - zl, zl)
    prev_dev = (zprev, 1 - core, x, y, zlprev)
    znext = jnp.where(core == 1, 1 - zh, zh)
    zlnext = jnp.where(core == 1, 1 - zl, zl)
    next_dev = (znext, 1 - core, x, y, zlnext)

    barrier = pltpu.get_barrier_semaphore()
    peers = []
    for i in (1, 2, 3):
        for o in (0, 1):
            peers.append(at(px=mod(x + i), pz=(zl + o) % 2))
            peers.append(at(py=mod(y + i), pz=(zl + o) % 2))
    cube = []
    for i in range(1, 8):
        cube.append(((zh + (i >> 2)) % 2, (core + ((i >> 1) & 1)) % 2, x, y, (zl + (i & 1)) % 2))
    for i in (1, 2, 3):
        for k in (1, 2, 3):
            peers.append(at(px=mod(x + i), py=mod(y + k)))
    peers += cube
    for p in peers:
        pl.semaphore_signal(barrier, inc=1, device_id=p, device_id_type=MESH)

    own = []
    for b in range(2):
        own.append(
            pltpu.make_async_copy(
                wave.at[b], W.at[b, x, y, pl.ds(pl.multiple_of(zl * ROWS, 8), ROWS), :], own_sem.at[b]
            )
        )
        own[-1].start()

    order = [6, 7, 2, 3, 4, 5, 0, 1]
    loads = []
    for n, i in enumerate(order):
        src = left if i < 4 else right
        j = i % 4
        loads.append(pltpu.make_async_copy(src.at[j // 2, j % 2], stage.at[n % 3], load_sem.at[n % 3]))
    for n in range(3):
        loads[n].start()
    fetch = [
        pltpu.make_async_copy(wave, wv, in_sem.at[0]),
        pltpu.make_async_copy(onsite, on_, in_sem.at[1]),
    ]
    for c in fetch:
        c.start()

    def split_op(n):
        i = order[n]
        hi_ref, lo_ref = (lh, ll) if i < 4 else (rh, rl)
        j = i % 4
        loads[n].wait()
        c = coup[j // 2, j % 2].astype(F32)

        def body(t, carry):
            rows = pl.ds(pl.multiple_of(t * 96, 16), 96)
            v = stage[n % 3, rows, :]
            if i < 4:
                v = v * c
            hi, lo = split(v)
            hi_ref[j, rows, :] = hi
            lo_ref[j, rows, :] = lo
            return carry

        lax.fori_loop(0, 8, body, 0)
        if n + 3 < 8:
            loads[n + 3].start()

    def lanes(h):
        return pl.ds(h * HALF, HALF)

    def spot(h, a, b):
        return (a, b) if h == 0 else (b, a)

    def rows_of(z):
        return pl.ds(pl.multiple_of(z * ROWS, 8), ROWS)

    hand = net.new(lambda: wave.at[0], lambda: W.at[2, x, y, rows_of(zl), :], prev_dev, 0)
    first_z = jnp.where(core == 1, 1 - zl, zl)

    class Gather:
        def __init__(self, blk, h):
            self.blk, self.h = blk, h
            a, b = (x, y) if h == 0 else (y, x)

            def slab(pa, pb):
                px, py = spot(h, pa, pb)
                return lambda: W.at[blk, px, py, :, lanes(h)]

            def dev(pa, pb, z=None):
                px, py = spot(h, pa, pb)
                return at(px=px, py=py, pz=z)

            z = first_z if blk == 2 else zl
            self.z = net.new(
                (lambda: W.at[2, x, y, rows_of(z), lanes(h)]) if blk == 2 else (lambda: wave.at[blk, :, lanes(h)]),
                lambda: W.at[blk, x, y, rows_of(z), lanes(h)],
                at(pz=1 - zl),
                0,
            )
            mine = slab(a, b)
            self.near = [None] + [net.new(mine, mine, dev(mod(a + i), b), 1) for i in (1, 2, 3)]
            fb, bb = dev(a, mod(b + d)), dev(a, mod(b - d))
            self.cols = []
            for o in range(4):
                pa = mod(a - o)
                s, t = slab(pa, b), slab(pa, mod(b - d))
                both = net.new_recv()
                self.cols.append((net.new(s, s, fb, 2), net.new(s, s, bb, 2, both), net.new(t, t, fb, 2, both), both))

        def spread(self, o):
            if o == 0:
                self.z.wait_recv()
                for i in (1, 3, 2):
                    self.near[i].start()
            else:
                self.near[o].wait_recv()
            self.cols[o][0].start()
            self.cols[o][1].start()

        def relay(self, o):
            self.cols[o][0].wait_recv()
            self.cols[o][2].start()

        def finish(self, o):
            wait_bytes(recv.at[self.cols[o][3]], rbB.at[0, 0, pl.ds(0, 2)])

    G1 = Gather(1, 0), Gather(1, 1)
    G0 = Gather(0, 0), Gather(0, 1)
    G2 = Gather(2, 0), Gather(2, 1)

    class Scatter:
        def __init__(self, blk, h):
            self.blk, self.h = blk, h
            a, b = (x, y) if h == 0 else (y, x)
            self.a, self.b = a, b
            u = blk * 2 + h
            self.u = u

            def slab(pa, pb):
                px, py = spot(h, pa, pb)
                return lambda: Pb.at[blk, px, py, :, lanes(h)]

            def dev(pa, pb, z=None):
                px, py = spot(h, pa, pb)
                return at(px=px, py=py, pz=z)

            self.slab = slab

            def buf(o, s):
                return lambda: rbB.at[u, o, s]

            self.rb = lambda o, s: rbB.at[u, o, s]
            fb, bb = dev(a, mod(b + d)), dev(a, mod(b - d))
            self.cols = []
            for o in range(4):
                both = net.new_recv()
                self.cols.append(
                    (
                        net.new(slab(o, mod(b + 2)), buf(o, 0), fb, 3),
                        net.new(slab(o, mod(b - d)), buf(o, 1), bb, 3, both),
                        net.new(slab(o, mod(b + d)), buf(o, 2), fb, 3, both),
                        both,
                    )
                )
            self.near, self.got = [], net.new_recv()
            for o in range(4):
                px, py = spot(h, o, b)
                for k in (1, 0):
                    z = (zl + k) % 2

                    def src(px=px, py=py, z=z):
                        return Pb.at[blk, px, py, rows_of(z), lanes(h)]

                    def dst(k=k):
                        return rbZ.at[u, a * 2 + k]

                    self.near.append(
                        net.new(src, dst, dev(o, b, z), 4, self.got, sends=None if k else a != o)
                    )

        def first(self, o, half):
            c = self.cols[o]
            if half is None or (self.h == 0 and o // 2 == half):
                c[0].start()
                c[1].start()
            elif self.h == 0:
                pass
            else:
                pl.when(lax.div(mod(self.b + 2), 2) == half)(c[0].start)
                pl.when(lax.div(mod(self.b - d), 2) == half)(c[1].start)

        def relay(self, o):
            c = self.cols[o]
            c[0].wait_recv()
            s = self.slab(o, mod(self.b + d))()
            s[...] = s[...] + self.rb(o, 0)[...]
            c[2].start()

        def land(self, o):
            c = self.cols[o]
            wait_bytes(recv.at[c[3]], rbB.at[self.u, o, pl.ds(1, 2)])
            s = self.slab(o, self.b)()
            s[...] = s[...] + self.rb(o, 1)[...] + self.rb(o, 2)[...]
            self.near[2 * o].start()
            self.near[2 * o + 1].start()

        def result(self):
            wait_bytes(recv.at[self.got], rbZ.at[self.u, pl.ds(1, 7)])
            rbZ[self.u, self.a * 2] = Pb[self.blk, x, y, rows_of(zl), lanes(self.h)]
            t = rbZ[self.u, 0]
            for k in range(1, 8):
                t = t + rbZ[self.u, k]
            return t

    S1 = Scatter(1, 0), Scatter(1, 1)
    S0 = Scatter(0, 0), Scatter(0, 1)

    ex = [
        net.new((lambda q=q: Pb.at[2, (1 - zl) * 2 + q]), (lambda q=q: zin.at[q]), at(pz=1 - zl), 5, sends=core == 1)
        for q in range(2)
    ]
    pin_got = net.new_recv()
    far = [
        net.new((lambda q=q: zin.at[q]), (lambda q=q: pin.at[zl * 2 + q]), next_dev, 5, pin_got)
        for q in range(2)
    ]
    chip = [
        net.new((lambda q=q: Pb.at[2, q]), (lambda q=q: pin.at[q]), next_dev, 5, pin_got, sends=core == 0)
        for q in range(4)
    ]

    def take_pin(c):
        @pl.when(core == c)
        def _():
            n = 4 if c else 2
            wait_bytes(recv.at[pin_got], pin.at[pl.ds(0, n)])

            def add(i, carry):
                k = i if c else (1 - zl) * 2 + i
                Pb[0, k] = Pb[0, k] + pin[k]
                return carry

            lax.fori_loop(0, n, add, 0)
            for u in S0:
                for o in range(4):
                    u.first(o, None)

    def give(first):
        for c in ex if first else chip:
            c.start()

    def fold_pair(q):
        @pl.when(core == 1)
        def _():
            ex[q].desc().wait_recv()
            zin[q] = zin[q] + Pb[2, zl * 2 + q]
            far[q].desc().start()

    plane = []
    for i in range(RING):
        for k in range(RING):
            if (i, k) != (0, 0):
                plane.append(at(px=mod(x + i), py=mod(y + k)))
    GX = ([at(px=mod(x + i)) for i in (1, 2, 3)], x)
    GY = ([at(py=mod(y + i)) for i in (1, 2, 3)], y)
    GC = (cube, zh * 4 + core * 2 + zl)
    GP = (plane, x * RING + y)

    class Total:
        def __init__(self, base, groups):
            self.stages = []
            for devs, me in groups:
                n = len(devs) + 1
                got = net.new_recv()

                def spot_of(base=base, me=me):
                    return red.at[base + me]

                copies = [net.new(spot_of, spot_of, p, 6, got) for p in devs]
                self.stages.append((base, n, spot_of, copies, got))
                base += n
            self.end = base

        def put(self, k, pair):
            _, _, spot_of, copies, _ = self.stages[k]
            r = spot_of()
            r[...] = pair
            for c in copies:
                c.start()

        def get(self, k):
            base, n, _, copies, got = self.stages[k]
            wait_bytes(recv.at[got], red.at[pl.ds(0, n - 1)])
            s = red[base]
            for i in range(1, n):
                s = s + red[base + i]
            return s

        def step(self, k):
            self.put(k + 1, self.get(k))

        def done(self):
            s = self.get(len(self.stages) - 1)
            return jnp.sum(s[0], keepdims=True), jnp.sum(s[1], keepdims=True)

    def stage1(blk, j, transposed, hooks, at_u=0):
        def body(i, carry):
            for n, hook in enumerate(hooks):
                pl.when(i == n)(hook)
            m = lax.rem(i, 2)
            k = lax.div(i, 2)
            w = split(W[blk, pl.ds(2 * m, 2)].reshape(HALF, M))
            r = (rh[2 * j + k], rl[2 * j + k])
            u = split(dot3(w, r, NT if transposed else NN))
            rows = pl.ds(pl.multiple_of(m * HALF, HALF), HALF)
            uh[at_u + k, rows, :] = u[0]
            ul[at_u + k, rows, :] = u[1]
            return carry

        lax.fori_loop(0, 4, body, 0)

    def stage2(parts, hooks, put, flip=None):
        def body(i, carry):
            m = i if flip is None else jnp.where(flip, 1 - i, i)
            cut = pl.ds(pl.multiple_of(m * HALF, HALF), HALF)
            total = None
            for n, hook in enumerate(hooks):
                if hook is not none:
                    pl.when(i == n)(hook)
            for j, transposed, at_u in parts:
                for k in range(2):
                    if transposed:
                        a = (lh[2 * j + k, :, cut], ll[2 * j + k, :, cut])
                    else:
                        a = (lh[2 * j + k, cut, :], ll[2 * j + k, cut, :])
                    t = dot3(a, (uh[at_u + k], ul[at_u + k]), TN if transposed else NN)
                    total = t if total is None else total + t
            put(m, total.reshape(2, RING, SLAB, M))
            return carry

        lax.fori_loop(0, 2, body, 0)

    def none():
        pass

    def put_to(blk):
        def put(m, v):
            Pb[blk, pl.ds(2 * m, 2)] = v

        return put

    def inner(wblk, pblk):
        def body(i, acc):
            return acc + fold((W[wblk, i] * Pb[pblk, i]).reshape(RING * SLAB, M))

        return lax.fori_loop(0, 4, body, jnp.zeros((8, 128), F32))

    def on(pair, fn):
        def run():
            for g in pair:
                fn(g)

        return run

    def send_half(pair, half):
        for s in pair:
            for o in range(4):
                s.first(o, half)

    def land(pair, cols):
        for o in cols:
            for s in pair:
                s.land(o)

    def do(*acts):
        def run():
            for a in acts:
                a()

        return run

    def spread(pair, *cols):
        return lambda: [on(pair, lambda g: g.spread(o))() for o in cols] and None

    def relay(pair, *cols):
        return lambda: [on(pair, lambda g: g.relay(o))() for o in cols] and None

    def finish(pair, *cols):
        return lambda: [on(pair, lambda g: g.finish(o))() for o in cols] and None

    pl.semaphore_wait(barrier, len(peers))
    for g in G1:
        g.z.start()
    hand.start()
    for g in G0:
        g.z.start()
    own[0].wait()
    own[1].wait()
    split_op(0)
    spread(G1, 0)()
    split_op(1)
    split_op(2)
    spread(G1, 1, 3)()
    split_op(3)
    spread(G1, 2)()
    split_op(4)
    hand.wait_recv()
    for g in G2:
        g.z.start()
    relay(G1, 0)()
    split_op(5)
    relay(G1, 1)()
    split_op(6)
    relay(G1, 3)()
    split_op(7)
    relay(G1, 2)()
    spread(G0, 0)()
    finish(G1, 0, 1, 3, 2)()
    stage1(1, 1, True, [none, spread(G0, 1, 3), spread(G0, 2), relay(G0, 0)])
    stage2(
        [(1, False, 0)],
        [relay(G0, 1, 3), do(lambda: give(True), relay(G0, 2))],
        put_to(2),
        zl == 0,
    )
    give(False)
    stage1(
        1, 0, False,
        [do(finish(G0, 0, 1), spread(G2, 0)), finish(G0, 3, 2), none, spread(G2, 1, 3)],
    )
    stage2([(0, True, 0)], [do(lambda: fold_pair(0), spread(G2, 2)), relay(G2, 0)], put_to(0))
    for c in fetch:
        c.wait()
    pp = fold(wv[0] * wv[0]) + fold(wv[1] * wv[1])
    ps = fold(on_[0] * wv[0] * wv[0]) + fold(on_[1] * wv[1] * wv[1])
    ps = ps + 2.0 * inner(0, 0)
    fold_pair(1)
    take_pin(1)
    stage1(0, 0, True, [relay(G2, 1), relay(G2, 3), relay(G2, 2)])
    finish(G2, 0, 1, 3, 2)()
    ps = ps + 2.0 * inner(2, 2)
    t0 = Total(0, (GX, GY, GC))
    t1 = Total(16, (GP, GC))
    t0.put(0, jnp.stack([pp, ps]))

    def early(*acts):
        return lambda: pl.when(core == 1)(do(*acts))

    def late(*acts):
        return lambda: pl.when(core == 0)(do(*acts))

    stage1(2, 1, False, [none, early(relay(S0, 0, 1, 2, 3)), lambda: take_pin(0)], 2)
    stage2(
        [(0, False, 0), (1, True, 2)],
        [
            do(lambda: t0.step(0), early(lambda: land(S0, range(4)))),
            do(lambda: send_half(S1, 0), lambda: t0.step(1), late(relay(S0, 0, 1, 2, 3))),
        ],
        put_to(1),
    )
    send_half(S1, 1)
    relay(S1[:1], 0, 1)()
    late(lambda: land(S0, range(4)))()
    norm_sq, energy_sum = t0.done()
    energy = energy_sum / norm_sq
    out = []

    def close(b, pair, pt, tt):
        for s in pair:
            h = slice(s.h * HALF, s.h * HALF + HALF)
            w, o_ = wv[b, :, h], on_[b, :, h]
            total = s.result()
            ob[0, b, :, h] = total
            sig = o_ * w + total
            gap = o_ - energy
            first = (sig - energy * w) * gap / jnp.maximum(gap * gap, 1.0)
            ob[1, b, :, h] = first
            pt = pt + fold(w * first)
            tt = tt + fold(first * first)
        out.append(pltpu.make_async_copy(ob.at[0, b], psum_out.at[b], out_sem.at[b]))
        out.append(pltpu.make_async_copy(ob.at[1, b], first_out.at[b], out_sem.at[2 + b]))
        return pt, tt

    relay(S1[1:], 0, 1, 2, 3)()
    relay(S1[:1], 2, 3)()
    land(S1[:1], (0, 1))
    land(S1[1:], (0, 1, 2, 3))
    land(S1[:1], (2, 3))
    zero = jnp.zeros((8, 128), F32)
    pt, tt = close(0, S0, zero, zero)
    pt, tt = close(1, S1, pt, tt)
    t1.put(0, jnp.stack([pt, tt]))
    for c in out:
        c.start()
    t1.step(0)
    correlation, first_sq = t1.done()
    ratio = correlation / norm_sq
    length_sq = first_sq - correlation * ratio
    ratio_out[...] = jnp.broadcast_to(ratio, (ROWS, M))
    scale_out[...] = jnp.broadcast_to(lax.rsqrt(length_sq / float(8 * M * M) + 1e-06), (ROWS, M))
    for c in out:
        c.wait()
    slabs = Pb.at[:, :, :, :, lanes(0)]
    waits = (
        rbZ.at[0],
        rbB.at[pl.ds(0, 3), pl.ds(0, 2)],
        Pb.at[:, :, pl.ds(0, 3)],
        slabs,
        rbZ.at[:, pl.ds(1, 7)],
        pin,
        red.at[pl.ds(0, 35)],
    )
    for group, like in enumerate(waits):
        wait_bytes(send.at[group], like)


def solution(mesh):
    finer = Mesh(mesh.devices.reshape(2, 2, 4, 4, 2), AXES)
    block = P(SECTOR, OP, None)
    ops = P(SECTOR, OP, None, None)

    def step(wave, onsite, left, right, coupling):
        vm = pl.BlockSpec(memory_space=pltpu.VMEM)
        anyw = pl.BlockSpec(memory_space=pl.ANY)
        shape = jax.ShapeDtypeStruct((2, ROWS, M), F32)
        psum, first, ratio, scale = pl.pallas_call(
            kernel,
            out_shape=(shape, shape) + (jax.ShapeDtypeStruct((ROWS, M), F32),) * 2,
            in_specs=[anyw, anyw, anyw, anyw, pl.BlockSpec(memory_space=pltpu.SMEM)],
            out_specs=(anyw, anyw, vm, vm),
            scratch_shapes=[
                pltpu.VMEM((4, M, M), BF16),
                pltpu.VMEM((4, M, M), BF16),
                pltpu.VMEM((4, M, M), BF16),
                pltpu.VMEM((4, M, M), BF16),
                pltpu.VMEM((3, M, M), F32),
                pltpu.VMEM((3, RING, RING, SLAB, M), F32),
                pltpu.VMEM((4, M, M), BF16),
                pltpu.VMEM((4, M, M), BF16),
                pltpu.VMEM((3, RING, RING, SLAB, M), F32),
                pltpu.VMEM((RING, RING, SLAB, M), F32),
                pltpu.VMEM((2, RING, SLAB, M), F32),
                pltpu.VMEM((4, 4, 3, SLAB, HALF), F32),
                pltpu.VMEM((4, 8, ROWS, HALF), F32),
                pltpu.VMEM((40, 2, 8, 128), F32),
                pltpu.VMEM((2, ROWS, M), F32),
                pltpu.VMEM((2, ROWS, M), F32),
                pltpu.VMEM((2, 2, ROWS, M), F32),
                pltpu.SemaphoreType.DMA((3,)),
                pltpu.SemaphoreType.DMA((2,)),
                pltpu.SemaphoreType.DMA((2,)),
                pltpu.SemaphoreType.DMA((4,)),
                pltpu.SemaphoreType.DMA((N_SEND,)),
                pltpu.SemaphoreType.DMA((N_RECV,)),
            ],
            compiler_params=pltpu.CompilerParams(
                collective_id=0, has_side_effects=True, vmem_limit_bytes=67043328
            ),
        )(wave, onsite, left, right, coupling)
        sigma = onsite * wave + psum
        return sigma, (first - ratio * wave) * scale

    return jax.shard_map(
        step,
        mesh=finer,
        in_specs=(block, block, ops, ops, P(SECTOR, OP)),
        out_specs=(block, block),
        check_vma=False,
    )
```

```python
import functools

import jax
import jax.numpy as jnp
from jax import lax
from jax.experimental import pallas as pl
from jax.experimental.pallas import tpu as pltpu
from jax.sharding import Mesh
from jax.sharding import PartitionSpec as P

AXES = ("zh", "core", "x", "y", "zl")
SECTOR = ("zh", "core")
OP = ("x", "y", "zl")
MESH = pl.DeviceIdType.MESH
F32 = jnp.float32
BF16 = jnp.bfloat16
M = 768
RING = 4
SLAB = 48
ROWS = 24
HALF = 384
N_SEND = 7
N_RECV = 120


def split(v):
    hi = v.astype(BF16)
    return hi, (v - hi.astype(F32)).astype(BF16)


def dot3(a, b, dims):
    def one(p, q):
        return lax.dot_general(p, q, (dims, ((), ())), preferred_element_type=F32)

    return one(a[0], b[0]) + one(a[0], b[1]) + one(a[1], b[0])


NN = ((1,), (0,))
NT = ((1,), (1,))
TN = ((0,), (0,))


def fold(v):
    t = v.reshape(-1, 8, v.shape[-1]).sum(0)
    out = t[:, 0:128]
    for i in range(1, v.shape[-1] // 128):
        out = out + t[:, 128 * i : 128 * (i + 1)]
    return out


class Copies:
    def __init__(self, send, recv):
        self.send, self.recv, self.got = send, recv, 0

    def new_recv(self):
        assert self.got < N_RECV
        self.got += 1
        return self.got - 1

    def new(self, src, dst, dev, group, got=None, sends=None, gets=None):
        return Copy(self, src, dst, dev, group, self.new_recv() if got is None else got, sends, gets)


class Copy:
    def __init__(self, net, src, dst, dev, group, got, sends, gets):
        self.net, self.src, self.dst, self.dev = net, src, dst, dev
        self.group, self.got, self.sends, self.gets = group, got, sends, gets

    def desc(self):
        return pltpu.make_async_remote_copy(
            src_ref=self.src(),
            dst_ref=self.dst(),
            send_sem=self.net.send.at[self.group],
            recv_sem=self.net.recv.at[self.got],
            device_id=self.dev,
            device_id_type=MESH,
        )

    def under(self, cond, act):
        if cond is None:
            act(self.desc())
        else:
            pl.when(cond)(lambda: act(self.desc()))

    def start(self):
        self.under(self.sends, lambda c: c.start())

    def wait_recv(self):
        self.under(self.gets, lambda c: c.wait_recv())


def wait_bytes(sem, like):
    pltpu.make_async_copy(like, like, sem).wait()


def kernel(
    wave, onsite, left, right, coup,
    psum_out, first_out, ratio_out, scale_out,
    lh, ll, rh, rl, stage, W, uh, ul, Pb, pin, zin, rbB, rbZ, red, wv, on_, ob,
    load_sem, own_sem, in_sem, out_sem, send, recv,
):
    zh, core, x, y, zl = (lax.axis_index(a) for a in AXES)
    net = Copies(send, recv)
    d = 1 - 2 * core

    def at(px=None, py=None, pz=None):
        return (zh, core, x if px is None else px, y if py is None else py, zl if pz is None else pz)

    def mod(v):
        return lax.rem(v + 8, RING)

    zprev = jnp.where(core == 0, 1 - zh, zh)
    zlprev = jnp.where(core == 0, 1 - zl, zl)
    prev_dev = (zprev, 1 - core, x, y, zlprev)
    znext = jnp.where(core == 1, 1 - zh, zh)
    zlnext = jnp.where(core == 1, 1 - zl, zl)
    next_dev = (znext, 1 - core, x, y, zlnext)

    barrier = pltpu.get_barrier_semaphore()
    peers = []
    for i in (1, 2, 3):
        for o in (0, 1):
            peers.append(at(px=mod(x + i), pz=(zl + o) % 2))
            peers.append(at(py=mod(y + i), pz=(zl + o) % 2))
    cube = []
    for i in range(1, 8):
        cube.append(((zh + (i >> 2)) % 2, (core + ((i >> 1) & 1)) % 2, x, y, (zl + (i & 1)) % 2))
    for i in (1, 2, 3):
        for k in (1, 2, 3):
            peers.append(at(px=mod(x + i), py=mod(y + k)))
    peers += cube
    for p in peers:
        pl.semaphore_signal(barrier, inc=1, device_id=p, device_id_type=MESH)

    own = []
    for b in range(2):
        own.append(
            pltpu.make_async_copy(
                wave.at[b], W.at[b, x, y, pl.ds(pl.multiple_of(zl * ROWS, 8), ROWS), :], own_sem.at[b]
            )
        )
        own[-1].start()

    order = [6, 7, 2, 3, 4, 5, 0, 1]
    loads = []
    for n, i in enumerate(order):
        src = left if i < 4 else right
        j = i % 4
        loads.append(pltpu.make_async_copy(src.at[j // 2, j % 2], stage.at[n % 3], load_sem.at[n % 3]))
    for n in range(3):
        loads[n].start()
    fetch = [
        pltpu.make_async_copy(wave, wv, in_sem.at[0]),
        pltpu.make_async_copy(onsite, on_, in_sem.at[1]),
    ]
    for c in fetch:
        c.start()

    def split_op(n):
        i = order[n]
        hi_ref, lo_ref = (lh, ll) if i < 4 else (rh, rl)
        j = i % 4
        loads[n].wait()
        c = coup[j // 2, j % 2].astype(F32)

        def body(t, carry):
            rows = pl.ds(pl.multiple_of(t * 96, 16), 96)
            v = stage[n % 3, rows, :]
            if i < 4:
                v = v * c
            hi, lo = split(v)
            hi_ref[j, rows, :] = hi
            lo_ref[j, rows, :] = lo
            return carry

        lax.fori_loop(0, 8, body, 0)
        if n + 3 < 8:
            loads[n + 3].start()

    def lanes(h):
        return pl.ds(h * HALF, HALF)

    def spot(h, a, b):
        return (a, b) if h == 0 else (b, a)

    def rows_of(z):
        return pl.ds(pl.multiple_of(z * ROWS, 8), ROWS)

    hand = net.new(lambda: wave.at[0], lambda: W.at[2, x, y, rows_of(zl), :], prev_dev, 0)
    first_z = jnp.where(core == 1, 1 - zl, zl)

    class Gather:
        def __init__(self, blk, h):
            self.blk, self.h = blk, h
            a, b = (x, y) if h == 0 else (y, x)

            def slab(pa, pb):
                px, py = spot(h, pa, pb)
                return lambda: W.at[blk, px, py, :, lanes(h)]

            def dev(pa, pb, z=None):
                px, py = spot(h, pa, pb)
                return at(px=px, py=py, pz=z)

            z = first_z if blk == 2 else zl
            self.z = net.new(
                (lambda: W.at[2, x, y, rows_of(z), lanes(h)]) if blk == 2 else (lambda: wave.at[blk, :, lanes(h)]),
                lambda: W.at[blk, x, y, rows_of(z), lanes(h)],
                at(pz=1 - zl),
                0,
            )
            mine = slab(a, b)
            self.near = [None] + [net.new(mine, mine, dev(mod(a + i), b), 1) for i in (1, 2, 3)]
            fb, bb = dev(a, mod(b + d)), dev(a, mod(b - d))
            self.cols = []
            for o in range(4):
                pa = mod(a - o)
                s, t = slab(pa, b), slab(pa, mod(b - d))
                both = net.new_recv()
                self.cols.append((net.new(s, s, fb, 2), net.new(s, s, bb, 2, both), net.new(t, t, fb, 2, both), both))

        def spread(self, o):
            if o == 0:
                self.z.wait_recv()
                for i in (1, 3, 2):
                    self.near[i].start()
            else:
                self.near[o].wait_recv()
            self.cols[o][0].start()
            self.cols[o][1].start()

        def relay(self, o):
            self.cols[o][0].wait_recv()
            self.cols[o][2].start()

        def finish(self, o):
            wait_bytes(recv.at[self.cols[o][3]], rbB.at[0, 0, pl.ds(0, 2)])

    G1 = Gather(1, 0), Gather(1, 1)
    G0 = Gather(0, 0), Gather(0, 1)
    G2 = Gather(2, 0), Gather(2, 1)

    class Scatter:
        def __init__(self, blk, h):
            self.blk, self.h = blk, h
            a, b = (x, y) if h == 0 else (y, x)
            self.a, self.b = a, b
            u = blk * 2 + h
            self.u = u

            def slab(pa, pb):
                px, py = spot(h, pa, pb)
                return lambda: Pb.at[blk, px, py, :, lanes(h)]

            def dev(pa, pb, z=None):
                px, py = spot(h, pa, pb)
                return at(px=px, py=py, pz=z)

            self.slab = slab

            def buf(o, s):
                return lambda: rbB.at[u, o, s]

            self.rb = lambda o, s: rbB.at[u, o, s]
            fb, bb = dev(a, mod(b + d)), dev(a, mod(b - d))
            self.cols = []
            for o in range(4):
                both = net.new_recv()
                self.cols.append(
                    (
                        net.new(slab(o, mod(b + 2)), buf(o, 0), fb, 3),
                        net.new(slab(o, mod(b - d)), buf(o, 1), bb, 3, both),
                        net.new(slab(o, mod(b + d)), buf(o, 2), fb, 3, both),
                        both,
                    )
                )
            self.near, self.got = [], net.new_recv()
            for o in range(4):
                px, py = spot(h, o, b)
                for k in (1, 0):
                    z = (zl + k) % 2

                    def src(px=px, py=py, z=z):
                        return Pb.at[blk, px, py, rows_of(z), lanes(h)]

                    def dst(k=k):
                        return rbZ.at[u, a * 2 + k]

                    self.near.append(
                        net.new(src, dst, dev(o, b, z), 4, self.got, sends=None if k else a != o)
                    )

        def first(self, o, half):
            c = self.cols[o]
            if half is None or (self.h == 0 and o // 2 == half):
                c[0].start()
                c[1].start()
            elif self.h == 0:
                pass
            else:
                pl.when(lax.div(mod(self.b + 2), 2) == half)(c[0].start)
                pl.when(lax.div(mod(self.b - d), 2) == half)(c[1].start)

        def relay(self, o):
            c = self.cols[o]
            c[0].wait_recv()
            s = self.slab(o, mod(self.b + d))()
            s[...] = s[...] + self.rb(o, 0)[...]
            c[2].start()

        def land(self, o):
            c = self.cols[o]
            wait_bytes(recv.at[c[3]], rbB.at[self.u, o, pl.ds(1, 2)])
            s = self.slab(o, self.b)()
            s[...] = s[...] + self.rb(o, 1)[...] + self.rb(o, 2)[...]
            self.near[2 * o].start()
            self.near[2 * o + 1].start()

        def result(self):
            wait_bytes(recv.at[self.got], rbZ.at[self.u, pl.ds(1, 7)])
            rbZ[self.u, self.a * 2] = Pb[self.blk, x, y, rows_of(zl), lanes(self.h)]
            t = rbZ[self.u, 0]
            for k in range(1, 8):
                t = t + rbZ[self.u, k]
            return t

    S1 = Scatter(1, 0), Scatter(1, 1)
    S0 = Scatter(0, 0), Scatter(0, 1)

    ex = [
        net.new((lambda q=q: Pb.at[2, (1 - zl) * 2 + q]), (lambda q=q: zin.at[q]), at(pz=1 - zl), 5, sends=core == 1)
        for q in range(2)
    ]
    pin_got = net.new_recv()
    far = [
        net.new((lambda q=q: zin.at[q]), (lambda q=q: pin.at[zl * 2 + q]), next_dev, 5, pin_got)
        for q in range(2)
    ]
    chip = [
        net.new((lambda q=q: Pb.at[2, q]), (lambda q=q: pin.at[q]), next_dev, 5, pin_got, sends=core == 0)
        for q in range(4)
    ]

    def take_pin(c):
        @pl.when(core == c)
        def _():
            n = 4 if c else 2
            wait_bytes(recv.at[pin_got], pin.at[pl.ds(0, n)])

            def add(i, carry):
                k = i if c else (1 - zl) * 2 + i
                Pb[0, k] = Pb[0, k] + pin[k]
                return carry

            lax.fori_loop(0, n, add, 0)
            for u in S0:
                for o in range(4):
                    u.first(o, None)

    def give(first):
        for c in ex if first else chip:
            c.start()

    def fold_pair(q):
        @pl.when(core == 1)
        def _():
            ex[q].desc().wait_recv()
            zin[q] = zin[q] + Pb[2, zl * 2 + q]
            far[q].desc().start()

    plane = []
    for i in range(RING):
        for k in range(RING):
            if (i, k) != (0, 0):
                plane.append(at(px=mod(x + i), py=mod(y + k)))
    GX = ([at(px=mod(x + i)) for i in (1, 2, 3)], x)
    GY = ([at(py=mod(y + i)) for i in (1, 2, 3)], y)
    GC = (cube, zh * 4 + core * 2 + zl)
    GP = (plane, x * RING + y)

    class Total:
        def __init__(self, base, groups):
            self.stages = []
            for devs, me in groups:
                n = len(devs) + 1
                got = net.new_recv()

                def spot_of(base=base, me=me):
                    return red.at[base + me]

                copies = [net.new(spot_of, spot_of, p, 6, got) for p in devs]
                self.stages.append((base, n, spot_of, copies, got))
                base += n
            self.end = base

        def put(self, k, pair):
            _, _, spot_of, copies, _ = self.stages[k]
            r = spot_of()
            r[...] = pair
            for c in copies:
                c.start()

        def get(self, k):
            base, n, _, copies, got = self.stages[k]
            wait_bytes(recv.at[got], red.at[pl.ds(0, n - 1)])
            s = red[base]
            for i in range(1, n):
                s = s + red[base + i]
            return s

        def step(self, k):
            self.put(k + 1, self.get(k))

        def done(self):
            s = self.get(len(self.stages) - 1)
            return jnp.sum(s[0], keepdims=True), jnp.sum(s[1], keepdims=True)

    def stage1(blk, j, transposed, hooks, at_u=0):
        def body(i, carry):
            for n, hook in enumerate(hooks):
                pl.when(i == n)(hook)
            m = lax.rem(i, 2)
            k = lax.div(i, 2)
            w = split(W[blk, pl.ds(2 * m, 2)].reshape(HALF, M))
            r = (rh[2 * j + k], rl[2 * j + k])
            u = split(dot3(w, r, NT if transposed else NN))
            rows = pl.ds(pl.multiple_of(m * HALF, HALF), HALF)
            uh[at_u + k, rows, :] = u[0]
            ul[at_u + k, rows, :] = u[1]
            return carry

        lax.fori_loop(0, 4, body, 0)

    def stage1_at(px, at_u, hooks=()):
        def body(k, carry):
            for n, hook in enumerate(hooks):
                pl.when(k == n)(hook)
            w = split(W[1, px].reshape(RING * SLAB, M))
            u = split(dot3(w, (rh[k], rl[k]), NN))
            rows = pl.ds(pl.multiple_of(px * RING * SLAB, RING * SLAB), RING * SLAB)
            uh[at_u + k, rows, :] = u[0]
            ul[at_u + k, rows, :] = u[1]
            return carry

        lax.fori_loop(0, 2, body, 0)

    def stage2(parts, hooks, put, flip=None):
        def body(i, carry):
            m = i if flip is None else jnp.where(flip, 1 - i, i)
            cut = pl.ds(pl.multiple_of(m * HALF, HALF), HALF)
            total = None
            for n, hook in enumerate(hooks):
                if hook is not none:
                    pl.when(i == n)(hook)
            for j, transposed, at_u in parts:
                for k in range(2):
                    if transposed:
                        a = (lh[2 * j + k, :, cut], ll[2 * j + k, :, cut])
                    else:
                        a = (lh[2 * j + k, cut, :], ll[2 * j + k, cut, :])
                    t = dot3(a, (uh[at_u + k], ul[at_u + k]), TN if transposed else NN)
                    total = t if total is None else total + t
            put(m, total.reshape(2, RING, SLAB, M))
            return carry

        lax.fori_loop(0, 2, body, 0)

    def none():
        pass

    def put_to(blk):
        def put(m, v):
            Pb[blk, pl.ds(2 * m, 2)] = v

        return put

    def inner(wblk, pblk):
        def body(i, acc):
            return acc + fold((W[wblk, i] * Pb[pblk, i]).reshape(RING * SLAB, M))

        return lax.fori_loop(0, 4, body, jnp.zeros((8, 128), F32))

    def on(pair, fn):
        def run():
            for g in pair:
                fn(g)

        return run

    def send_half(pair, half):
        for s in pair:
            for o in range(4):
                s.first(o, half)

    def land(pair, cols):
        for o in cols:
            for s in pair:
                s.land(o)

    def do(*acts):
        def run():
            for a in acts:
                a()

        return run

    def spread(pair, *cols):
        return lambda: [on(pair, lambda g: g.spread(o))() for o in cols] and None

    def relay(pair, *cols):
        return lambda: [on(pair, lambda g: g.relay(o))() for o in cols] and None

    def finish(pair, *cols):
        return lambda: [on(pair, lambda g: g.finish(o))() for o in cols] and None

    pl.semaphore_wait(barrier, len(peers))
    for g in G1:
        g.z.start()
    hand.start()
    for g in G0:
        g.z.start()
    own[0].wait()
    own[1].wait()
    split_op(0)
    spread(G1, 0)()
    split_op(1)
    split_op(2)
    spread(G1, 1, 3)()
    split_op(3)
    spread(G1, 2)()
    split_op(4)
    hand.wait_recv()
    for g in G2:
        g.z.start()
    relay(G1, 0)()
    split_op(5)
    relay(G1, 1)()
    split_op(6)
    relay(G1, 3)()
    split_op(7)
    relay(G1, 2)()
    spread(G0, 0)()
    finish(G1[:1], 0)()
    stage1_at(x, 2)
    finish(G1[:1], 1, 3)()
    stage1_at(mod(x - d), 2)
    finish(G1[:1], 2)()
    finish(G1[1:], 0, 1, 2, 3)()
    stage1(1, 1, True, [none, spread(G0, 1, 3), spread(G0, 2), relay(G0, 0)])
    stage2(
        [(1, False, 0)],
        [relay(G0, 1, 3), do(lambda: give(True), relay(G0, 2))],
        put_to(2),
        zl == 0,
    )
    give(False)
    stage1_at(mod(x + d), 2, [none, do(finish(G0, 0, 1), spread(G2, 0))])
    stage1_at(mod(x + 2), 2, [none, finish(G0, 3, 2)])
    stage2([(0, True, 2)], [spread(G2, 1, 3), do(lambda: fold_pair(0), spread(G2, 2))], put_to(0))
    for c in fetch:
        c.wait()
    pp = fold(wv[0] * wv[0]) + fold(wv[1] * wv[1])
    ps = fold(on_[0] * wv[0] * wv[0]) + fold(on_[1] * wv[1] * wv[1])
    ps = ps + 2.0 * inner(0, 0)
    take_pin(1)
    stage1(0, 0, True, [relay(G2, 0), do(relay(G2, 1), lambda: fold_pair(1)), relay(G2, 3), relay(G2, 2)])
    finish(G2, 0, 1, 3, 2)()
    ps = ps + 2.0 * inner(2, 2)
    t0 = Total(0, (GX, GY, GC))
    t1 = Total(16, (GP, GC))
    t0.put(0, jnp.stack([pp, ps]))

    def early(*acts):
        return lambda: pl.when(core == 1)(do(*acts))

    def late(*acts):
        return lambda: pl.when(core == 0)(do(*acts))

    stage1(2, 1, False, [none, early(relay(S0, 0, 1, 2, 3)), lambda: take_pin(0)], 2)
    stage2(
        [(0, False, 0), (1, True, 2)],
        [
            do(lambda: t0.step(0), early(lambda: land(S0, range(4)))),
            do(lambda: send_half(S1, 0), lambda: t0.step(1), late(relay(S0, 0, 1, 2, 3))),
        ],
        put_to(1),
    )
    send_half(S1, 1)
    relay(S1[:1], 0, 1)()
    late(lambda: land(S0, range(4)))()
    norm_sq, energy_sum = t0.done()
    energy = energy_sum / norm_sq
    out = []

    def close(b, pair, pt, tt):
        for s in pair:
            h = slice(s.h * HALF, s.h * HALF + HALF)
            w, o_ = wv[b, :, h], on_[b, :, h]
            total = s.result()
            ob[0, b, :, h] = total
            sig = o_ * w + total
            gap = o_ - energy
            first = (sig - energy * w) * gap / jnp.maximum(gap * gap, 1.0)
            ob[1, b, :, h] = first
            pt = pt + fold(w * first)
            tt = tt + fold(first * first)
        out.append(pltpu.make_async_copy(ob.at[0, b], psum_out.at[b], out_sem.at[b]))
        out.append(pltpu.make_async_copy(ob.at[1, b], first_out.at[b], out_sem.at[2 + b]))
        return pt, tt

    relay(S1[1:], 0, 1, 2, 3)()
    relay(S1[:1], 2, 3)()
    land(S1[:1], (0, 1))
    land(S1[1:], (0, 1, 2, 3))
    land(S1[:1], (2, 3))
    zero = jnp.zeros((8, 128), F32)
    pt, tt = close(0, S0, zero, zero)
    pt, tt = close(1, S1, pt, tt)
    t1.put(0, jnp.stack([pt, tt]))
    for c in out:
        c.start()
    t1.step(0)
    correlation, first_sq = t1.done()
    ratio = correlation / norm_sq
    length_sq = first_sq - correlation * ratio
    ratio_out[...] = jnp.broadcast_to(ratio, (ROWS, M))
    scale_out[...] = jnp.broadcast_to(lax.rsqrt(length_sq / float(8 * M * M) + 1e-06), (ROWS, M))
    for c in out:
        c.wait()
    slabs = Pb.at[:, :, :, :, lanes(0)]
    waits = (
        rbZ.at[0],
        rbB.at[pl.ds(0, 3), pl.ds(0, 2)],
        Pb.at[:, :, pl.ds(0, 3)],
        slabs,
        rbZ.at[:, pl.ds(1, 7)],
        pin,
        red.at[pl.ds(0, 35)],
    )
    for group, like in enumerate(waits):
        wait_bytes(send.at[group], like)


def solution(mesh):
    finer = Mesh(mesh.devices.reshape(2, 2, 4, 4, 2), AXES)
    block = P(SECTOR, OP, None)
    ops = P(SECTOR, OP, None, None)

    def step(wave, onsite, left, right, coupling):
        vm = pl.BlockSpec(memory_space=pltpu.VMEM)
        anyw = pl.BlockSpec(memory_space=pl.ANY)
        shape = jax.ShapeDtypeStruct((2, ROWS, M), F32)
        psum, first, ratio, scale = pl.pallas_call(
            kernel,
            out_shape=(shape, shape) + (jax.ShapeDtypeStruct((ROWS, M), F32),) * 2,
            in_specs=[anyw, anyw, anyw, anyw, pl.BlockSpec(memory_space=pltpu.SMEM)],
            out_specs=(anyw, anyw, vm, vm),
            scratch_shapes=[
                pltpu.VMEM((4, M, M), BF16),
                pltpu.VMEM((4, M, M), BF16),
                pltpu.VMEM((4, M, M), BF16),
                pltpu.VMEM((4, M, M), BF16),
                pltpu.VMEM((3, M, M), F32),
                pltpu.VMEM((3, RING, RING, SLAB, M), F32),
                pltpu.VMEM((4, M, M), BF16),
                pltpu.VMEM((4, M, M), BF16),
                pltpu.VMEM((3, RING, RING, SLAB, M), F32),
                pltpu.VMEM((RING, RING, SLAB, M), F32),
                pltpu.VMEM((2, RING, SLAB, M), F32),
                pltpu.VMEM((4, 4, 3, SLAB, HALF), F32),
                pltpu.VMEM((4, 8, ROWS, HALF), F32),
                pltpu.VMEM((40, 2, 8, 128), F32),
                pltpu.VMEM((2, ROWS, M), F32),
                pltpu.VMEM((2, ROWS, M), F32),
                pltpu.VMEM((2, 2, ROWS, M), F32),
                pltpu.SemaphoreType.DMA((3,)),
                pltpu.SemaphoreType.DMA((2,)),
                pltpu.SemaphoreType.DMA((2,)),
                pltpu.SemaphoreType.DMA((4,)),
                pltpu.SemaphoreType.DMA((N_SEND,)),
                pltpu.SemaphoreType.DMA((N_RECV,)),
            ],
            compiler_params=pltpu.CompilerParams(
                collective_id=0, has_side_effects=True, vmem_limit_bytes=67043328
            ),
        )(wave, onsite, left, right, coupling)
        sigma = onsite * wave + psum
        return sigma, (first - ratio * wave) * scale

    return jax.shard_map(
        step,
        mesh=finer,
        in_specs=(block, block, ops, ops, P(SECTOR, OP)),
        out_specs=(block, block),
        check_vma=False,
    )
```
